512 devices in a mesh: mode: 32 (over x_hi, z), slab: 16 (over x_lo, y, core).
Axes of the slice: x: 4 (x_hi: 2, x_lo: 2; x = x_hi * 2 + x_lo), y: 4, z: 16, core: 2. Of those that a mesh axis runs over, the one named last changes fastest.
Arguments:
- rhs: float32 [256, 5, 512, 128], P('mode', None, 'slab'), may hold values from -6 to 6
- start_state: float32 [256, 5, 512, 128], P('mode', None, 'slab'), may hold values from -6 to 6
- precond: bfloat16 [2, 5, 512, 5, 32], P(None, None, 'slab')
- coupling: float32 [2, 8, 5, 512], P(None, None, None, 'slab'), may hold values from -0.9 to 0.9
- edge_coef: float32 [5, 512], P(None, 'slab'), may hold values from 0.7 to 1.4
- harm_order: int32 [8], replicated, may hold values from 0 to 7, each once
Outputs:
- state: float32 [256, 5, 512, 128], P('mode', None, 'slab')
The draws below stay inside these ranges and needn't reach their ends.
Inputs may be any that keep to these rules, and one draw needn't show every extreme that they name: harm_order holds each of 0 to 7 once.
All inputs are finite; a program needn't handle non-finite values.
Results may differ from the reference program's by a relative error of at most 0.0037.
Values may be sent and summed in bfloat16 or wider, within the bound.
A program may use at most 64 MiB of HBM per device.

```python
import math
import jax
import jax.numpy as jnp
from jax import lax

MODES = 256
VARS = 5
SKETCH = 64
RAD_DEV = 32
NH = 8
HSTEP = 6
ITERS = 2
INNER = 1
RAD = 512
N_SLAB = 16


def draw_precond(key, part):
    key_noise = jax.random.fold_in(key, 11)
    row_pos = jnp.arange(RAD) % RAD_DEV
    col_pos = jnp.arange(RAD_DEV)
    distance = jnp.abs(row_pos[:, None] - col_pos[None, :]).astype(jnp.float32)
    diagonal = (row_pos[:, None] == col_pos[None, :]).astype(jnp.float32)
    corner_spot = (row_pos[:, None] == RAD_DEV - 1) & (col_pos[None, :] == 0)
    spread = 0.5 / math.sqrt(VARS * RAD_DEV)
    shape = (2, VARS, RAD, VARS, RAD_DEV)
    amplitude = 4.0
    corner = 0.85
    noise = jax.random.normal(key_noise, shape, jnp.float32) * spread
    smooth = diagonal + amplitude / RAD_DEV * jnp.exp(-distance / (2.0 * RAD_DEV))
    smooth = jnp.where(corner_spot, corner, smooth)
    same_var = jnp.eye(VARS, dtype=jnp.float32)
    base = same_var[:, None, :, None] * smooth[None, :, None, :]
    stacked = jnp.stack([base, jnp.zeros_like(base)], axis=0)
    return (stacked + noise).astype(jnp.bfloat16)


def shard_levels(own_key, dims, cuts, smallest, top_value):
    def one(axis_at, blocks):
        draws = jax.random.uniform(jax.random.fold_in(jax.random.fold_in(own_key, 6), axis_at), (blocks,), jnp.float32, smallest / len(cuts), top_value / len(cuts))
        return jnp.repeat(jnp.exp(draws), dims[axis_at] // blocks).reshape((-1,) + (1,) * (len(dims) - axis_at - 1))

    level = one(*cuts[0])
    for cut in cuts[1:]:
        level = level * one(*cut)
    return level


def gaussian(own_key, shape, scale, most, cuts=(), kind=jnp.bfloat16):
    factor_of = shard_levels(own_key, shape, cuts, -0.22, 0.18) if cuts else 1.0
    entries = jax.random.normal(own_key, shape, jnp.float32) * scale * factor_of
    return jnp.minimum(jnp.maximum(entries, -most), most).astype(kind)


def setup_inputs(seed: int = 0) -> dict:
    splits = jax.random.split(jax.random.key(seed), 7)
    rhs = gaussian(splits[0], (MODES, VARS, RAD, 2 * SKETCH), 1.0, 6.0, ((0, 32), (2, 16)), jnp.float32)
    start_state = gaussian(splits[1], (MODES, VARS, RAD, 2 * SKETCH), 1.0, 6.0, ((0, 32), (2, 16)), jnp.float32)
    precond = draw_precond(jax.random.fold_in(splits[6], 71), 0)
    coupling = gaussian(splits[3], (2, NH, VARS, RAD), 0.15, 0.9, ((3, 16),), jnp.float32)
    edge_coef = jnp.clip(jnp.exp(math.log(1.4) - 0.6931472 * jax.random.uniform(splits[4], (VARS, RAD), jnp.float32) ** shard_levels(splits[4], (VARS, RAD), ((1, 16),), -0.2, 0.2)), 0.7, 1.4)
    harm_order = jax.random.permutation(splits[5], NH).astype(jnp.int32)
    return {"rhs": rhs, "start_state": start_state, "precond": precond, "coupling": coupling, "edge_coef": edge_coef, "harm_order": harm_order}


def offsets_of(order):
    half = NH // 2
    return jnp.where(order < half, HSTEP * (order - half), HSTEP * (order - half + 1)).astype(jnp.int32)


def complex_scale(coef, field):
    half_cols = field.shape[-1] // 2
    coef_real = coef[0][None, :, :, None]
    coef_imag = coef[1][None, :, :, None]
    field_real = field[..., :half_cols]
    field_imag = field[..., half_cols:]
    return jnp.concatenate([coef_real * field_real - coef_imag * field_imag,
                            coef_real * field_imag + coef_imag * field_real], axis=-1)


def complex_apply(block, field):
    half_cols = field.shape[-1] // 2
    product = jnp.einsum('avrwt,mwtc->amvrc', block.astype(jnp.float32), field.astype(jnp.float32))
    real_part = product[0, ..., :half_cols] - product[1, ..., half_cols:]
    imag_part = product[0, ..., half_cols:] + product[1, ..., :half_cols]
    return jnp.concatenate([real_part, imag_part], axis=-1)


def slab_apply(precond, field):
    pieces = []
    for slab_index in range(N_SLAB):
        lower = slab_index * RAD_DEV
        pieces.append(complex_apply(precond[:, :, lower:lower + RAD_DEV], field[:, :, lower:lower + RAD_DEV]))
    return jnp.concatenate(pieces, axis=2)


def column_apply(column, pushed):
    half_cols = pushed.shape[-1] // 2
    push_real = pushed[..., :half_cols]
    push_imag = pushed[..., half_cols:]
    high = lax.Precision.HIGHEST
    real_part = (jnp.einsum('vrw,mwc->mvrc', column[0], push_real, precision=high)
                 - jnp.einsum('vrw,mwc->mvrc', column[1], push_imag, precision=high))
    imag_part = (jnp.einsum('vrw,mwc->mvrc', column[0], push_imag, precision=high)
                 + jnp.einsum('vrw,mwc->mvrc', column[1], push_real, precision=high))
    return jnp.concatenate([real_part, imag_part], axis=-1)


def reference(rhs, start_state, precond, coupling, edge_coef, harm_order):
    offsets = offsets_of(harm_order)
    reach = HSTEP * NH // 2
    cols = rhs.shape[-1]
    state = start_state
    gains = edge_coef.reshape(VARS, N_SLAB, RAD_DEV)
    for outer in range(ITERS):
        frozen = state.astype(jnp.bfloat16)
        padded = jnp.pad(frozen, ((reach, reach), (0, 0), (0, 0), (0, 0)))
        mixing = jnp.zeros(state.shape, jnp.float32)
        for index in range(NH):
            begin = (reach - offsets[index]).astype(jnp.int32)
            partner = lax.dynamic_slice_in_dim(padded, begin, MODES, 0)
            mixing = mixing + complex_scale(coupling[:, index], partner.astype(jnp.float32))
        forced = slab_apply(precond, mixing.astype(jnp.bfloat16))
        for inner in range(INNER):
            blocks = state.reshape(MODES, VARS, N_SLAB, RAD_DEV, cols)
            next_first = jnp.concatenate([blocks[:, :, 1:, 0], jnp.zeros((MODES, VARS, 1, cols), jnp.float32)], axis=2)
            lifted = rhs.reshape(MODES, VARS, N_SLAB, RAD_DEV, cols)
            last_rows = lifted[:, :, :, -1] + gains[None, :, :, -1, None] * next_first
            sweep_in = jnp.concatenate([lifted[:, :, :, :-1], last_rows[:, :, :, None]], axis=3)
            sweep_in = sweep_in.reshape(rhs.shape).astype(jnp.bfloat16)
            local = slab_apply(precond, sweep_in) - forced
            carried = jnp.zeros((MODES, VARS, cols), jnp.float32)
            pieces = []
            for slab_index in range(N_SLAB):
                lower = slab_index * RAD_DEV
                column = precond[:, :, lower:lower + RAD_DEV, :, 0].astype(jnp.float32)
                pushed = edge_coef[:, lower][None, :, None] * carried
                fresh = local[:, :, lower:lower + RAD_DEV] - column_apply(column, pushed)
                pieces.append(fresh)
                carried = fresh[:, :, -1]
            state = jnp.concatenate(pieces, axis=2)
    return state
```

```python
import functools

import jax
import jax.numpy as jnp
from jax import lax
from jax.experimental import pallas as pl
from jax.experimental.pallas import tpu as pltpu
from jax.sharding import PartitionSpec as P

NH = 8
HSTEP = 6
ITERS = 2
HALF = NH // 2
OFFS = [HSTEP * (k - HALF) if k < HALF else HSTEP * (k - HALF + 1) for k in range(NH)]
HOPS = 3
CHUNKS = 2
MESH = pl.DeviceIdType.MESH


def kernel(
    n_mode, n_slab,
    edge_ref, rhs_ref, start_ref, mat_ref, coef_ref, out_ref,
    frozen, halo, coef_b, col_b, trans, tails, rows_out, rows_in,
    base, acc_a, acc_b, mixed, edge_v, edge_j,
    halo_send, halo_recv, trans_send, trans_recv, tail_send, tail_recv, row_send, row_recv,
):
    modes = rhs_ref.shape[0]
    nrow = rhs_ref.shape[1]
    nvar = edge_ref.shape[0]
    rad = nrow // nvar
    part = modes // CHUNKS
    me = lax.axis_index("mode")
    slab = lax.axis_index("slab")
    lane = lax.broadcasted_iota(jnp.int32, (1, 128), 1)
    sign = jnp.where(lane < 64, -1.0, 1.0).astype(jnp.float32)

    def turn(x):
        return pltpu.roll(x, 64, x.ndim - 1) * sign

    barrier = pltpu.get_barrier_semaphore()
    for other in range(n_slab):
        @pl.when(other != slab)
        def _():
            pl.semaphore_signal(barrier, inc=1, device_id={"slab": other}, device_id_type=MESH)

    @pl.when(me > 0)
    def _():
        pl.semaphore_signal(barrier, inc=1, device_id={"mode": me - 1}, device_id_type=MESH)

    @pl.when(me < n_mode - 1)
    def _():
        pl.semaphore_signal(barrier, inc=1, device_id={"mode": me + 1}, device_id_type=MESH)

    frozen[0] = start_ref[...].astype(jnp.bfloat16)
    for v in range(nvar):
        rows_out[0, v] = start_ref[:, v * rad, :]

    n_near = jnp.where(me > 0, 1, 0) + jnp.where(me < n_mode - 1, 1, 0)
    pl.semaphore_wait(barrier, n_slab - 1 + n_near)

    def halo_copy(it, way, hop, c):
        cut = pl.ds(c * part, part)
        src = frozen.at[it, cut] if hop == 0 else halo.at[it, way, hop - 1, cut]
        to = me + 1 if way == 0 else me - 1
        return pltpu.make_async_remote_copy(
            src_ref=src,
            dst_ref=halo.at[it, way, hop, cut],
            send_sem=halo_send.at[it, way, hop, c],
            recv_sem=halo_recv.at[it, way, hop, c],
            device_id={"mode": to},
            device_id_type=MESH,
        )

    def sends(way, hop):
        if way == 0:
            return (me < n_mode - 1) & (me >= hop)
        return (me > 0) & (me + hop < n_mode)

    def gets(way, hop):
        return me >= hop + 1 if way == 0 else me + hop + 1 < n_mode

    def halo_start(it, hop, c):
        for way in range(2):
            @pl.when(sends(way, hop))
            def _():
                halo_copy(it, way, hop, c).start()

    def halo_wait(it, hop, c):
        for way in range(2):
            @pl.when(gets(way, hop))
            def _():
                halo_copy(it, way, hop, c).wait_recv()

    def row_copy(it):
        return pltpu.make_async_remote_copy(
            src_ref=rows_out.at[it], dst_ref=rows_in.at[it],
            send_sem=row_send.at[it], recv_sem=row_recv.at[it],
            device_id={"slab": slab - 1}, device_id_type=MESH,
        )

    def trans_copy(source, other):
        return pltpu.make_async_remote_copy(
            src_ref=trans.at[source], dst_ref=trans.at[source],
            send_sem=trans_send.at[other], recv_sem=trans_recv.at[source],
            device_id={"slab": other}, device_id_type=MESH,
        )

    def tail_copy(it, source, other):
        return pltpu.make_async_remote_copy(
            src_ref=tails.at[it, source], dst_ref=tails.at[it, source],
            send_sem=tail_send.at[it, other], recv_sem=tail_recv.at[it, source],
            device_id={"slab": other}, device_id_type=MESH,
        )

    for c in range(CHUNKS):
        halo_start(0, 0, c)

    @pl.when(slab > 0)
    def _():
        row_copy(0).start()

    for v in range(nvar):
        for p in range(2):
            col = mat_ref[p * nrow:(p + 1) * nrow, v * rad:v * rad + 1].astype(jnp.float32)
            col_b[p, v] = jnp.broadcast_to(col * edge_ref[v, 0], (nrow, 128))
    for p in range(2):
        for v in range(nvar):
            for w in range(nvar):
                row = v * rad + rad - 1
                trans[slab, pl.ds(p * nvar * nvar + v * nvar + w, 1)] = -col_b[p, w, row:row + 1, :]
    for other in range(1, n_slab):
        @pl.when(other > slab)
        def _():
            trans_copy(slab, other).start()
    for p in range(2):
        for k in range(NH):
            pick = coef_ref[:, p * NH + k:p * NH + k + 1]
            coef_b[p, k] = jnp.broadcast_to(pick, (nrow, 128))
    for it in range(ITERS):
        for hop in range(HOPS):
            for way in range(2):
                @pl.when(jnp.logical_not(gets(way, hop)))
                def _():
                    halo[it, way, hop] = jnp.zeros(halo.shape[3:], halo.dtype)

    @pl.when(slab == n_slab - 1)
    def _():
        rows_in[...] = jnp.zeros_like(rows_in)

    def product(x):
        both = jnp.dot(mat_ref[...], x, preferred_element_type=jnp.float32)
        return both[:nrow] + turn(both[nrow:])

    def accumulate(it, stage):
        def block(v, carry):
            cut = pl.ds(pl.multiple_of(v * rad, rad), rad)
            for m in range(modes):
                a = b = None
                if stage > 1:
                    a, b = acc_a[m, cut], acc_b[m, cut]
                for k in range(NH):
                    dist, src = divmod(m - OFFS[k], modes)
                    if max(1, abs(dist)) != stage:
                        continue
                    if dist == 0:
                        x = frozen[it, src, cut]
                    else:
                        x = halo[it, 0 if dist < 0 else 1, abs(dist) - 1, src, cut]
                    x = x.astype(jnp.float32)
                    ax, bx = coef_b[0, k, cut] * x, coef_b[1, k, cut] * x
                    a = ax if a is None else a + ax
                    b = bx if b is None else b + bx
                if stage == HOPS:
                    mixed[m, cut] = (a + turn(b)).astype(jnp.bfloat16)
                else:
                    acc_a[m, cut] = a
                    acc_b[m, cut] = b
            return carry

        lax.fori_loop(0, nvar, block, 0)

    last = lax.broadcasted_iota(jnp.int32, (rad, 1), 0) == rad - 1

    for it in range(ITERS):
        @pl.when(slab < n_slab - 1)
        def _():
            row_copy(it).wait_recv()

        for m in range(modes):
            pieces = []
            for v in range(nvar):
                x = rhs_ref[m, v * rad:(v + 1) * rad, :]
                nxt = edge_ref[v, rad - 1] * rows_in[it, v, m:m + 1, :]
                pieces.append(jnp.where(last, x + nxt, x).astype(jnp.bfloat16))
            base[m] = product(jnp.concatenate(pieces, axis=0))

        for hop in range(HOPS):
            for c in range(CHUNKS):
                halo_wait(it, hop, c)
                if hop + 1 < HOPS:
                    halo_start(it, hop + 1, c)
            accumulate(it, hop + 1)

        for m in range(modes):
            base[m] = base[m] - product(mixed[m])
        for v in range(nvar):
            tails[it, slab, v] = base[:, v * rad + rad - 1, :]
        for other in range(n_slab - 1, 0, -1):
            @pl.when(other > slab)
            def _():
                tail_copy(it, slab, other).start()

        def carry_on(j, edge):
            if it == 0:
                trans_copy(j, slab).wait_recv()
            tail_copy(it, j, slab).wait_recv()
            turned = [turn(e) for e in edge]
            fresh = []
            for v in range(nvar):
                total = tails[it, j, v]
                for w in range(nvar):
                    at = v * nvar + w
                    total = total + trans[j, pl.ds(at, 1)] * edge[w]
                    total = total + trans[j, pl.ds(nvar * nvar + at, 1)] * turned[w]
                fresh.append(total)
            return tuple(fresh)

        zero = jnp.zeros((modes, 128), jnp.float32)
        edge = lax.fori_loop(0, slab, carry_on, (zero,) * nvar)
        for w in range(nvar):
            edge_v[w] = edge[w]
            edge_j[w] = turn(edge[w])
        for m in range(modes):
            total = base[m]
            for w in range(nvar):
                total = total - col_b[0, w] * edge_v[w, m:m + 1, :]
                total = total - col_b[1, w] * edge_j[w, m:m + 1, :]
            if it == ITERS - 1:
                out_ref[m] = total
            else:
                frozen[it + 1, m] = total.astype(jnp.bfloat16)
                for v in range(nvar):
                    rows_out[it + 1, v, m:m + 1, :] = total[v * rad:v * rad + 1, :]
        if it < ITERS - 1:
            for c in range(CHUNKS):
                halo_start(it + 1, 0, c)

            @pl.when(slab > 0)
            def _():
                row_copy(it + 1).start()

    for other in range(1, n_slab):
        @pl.when(other > slab)
        def _():
            trans_copy(slab, other).wait_send()
            for it in range(ITERS):
                tail_copy(it, slab, other).wait_send()

    @pl.when(slab > 0)
    def _():
        for it in range(ITERS):
            row_copy(it).wait_send()

    for it in range(ITERS):
        for way in range(2):
            for hop in range(HOPS):
                @pl.when(sends(way, hop))
                def _():
                    for c in range(CHUNKS):
                        halo_copy(it, way, hop, c).wait_send()


def body(rhs, start_state, precond, coupling, edge_coef, harm_order):
    n_mode, n_slab = lax.axis_size("mode"), lax.axis_size("slab")
    modes, nvar, rad, cols = rhs.shape
    nrow = nvar * rad
    chosen = harm_order[None, :] == jnp.arange(NH)[:, None]
    ranked = jnp.sum(
        jnp.where(chosen[None, :, :, None, None], coupling[:, None], 0.0), axis=2
    )
    coefs = ranked.transpose(2, 3, 0, 1).reshape(nrow, 2 * NH)
    matrix = precond.reshape(2 * nrow, nrow)
    f32, bf16 = jnp.float32, jnp.bfloat16
    dma = pltpu.SemaphoreType.DMA
    vmem = pl.BlockSpec(memory_space=pltpu.VMEM)
    state = pl.pallas_call(
        functools.partial(kernel, n_mode, n_slab),
        out_shape=jax.ShapeDtypeStruct((modes, nrow, cols), f32),
        in_specs=[pl.BlockSpec(memory_space=pltpu.SMEM)] + [vmem] * 4,
        out_specs=vmem,
        scratch_shapes=[
            pltpu.VMEM((ITERS, modes, nrow, cols), bf16),
            pltpu.VMEM((ITERS, 2, HOPS, modes, nrow, cols), bf16),
            pltpu.VMEM((2, NH, nrow, 128), f32),
            pltpu.VMEM((2, nvar, nrow, 128), f32),
            pltpu.VMEM((n_slab, 56, 128), f32),
            pltpu.VMEM((ITERS, n_slab, nvar, modes, cols), f32),
            pltpu.VMEM((ITERS, nvar, modes, cols), f32),
            pltpu.VMEM((ITERS, nvar, modes, cols), f32),
            pltpu.VMEM((modes, nrow, cols), f32),
            pltpu.VMEM((modes, nrow, cols), f32),
            pltpu.VMEM((modes, nrow, cols), f32),
            pltpu.VMEM((modes, nrow, cols), bf16),
            pltpu.VMEM((nvar, modes, cols), f32),
            pltpu.VMEM((nvar, modes, cols), f32),
            dma((ITERS, 2, HOPS, CHUNKS)),
            dma((ITERS, 2, HOPS, CHUNKS)),
            dma((n_slab,)),
            dma((n_slab,)),
            dma((ITERS, n_slab)),
            dma((ITERS, n_slab)),
            dma((ITERS,)),
            dma((ITERS,)),
        ],
        compiler_params=pltpu.CompilerParams(
            collective_id=0, has_side_effects=True, vmem_limit_bytes=48 * 1024 * 1024
        ),
    )(edge_coef, rhs.reshape(modes, nrow, cols), start_state.reshape(modes, nrow, cols), matrix, coefs)
    return state.reshape(rhs.shape)


def solution(mesh):
    in_specs = (
        P("mode", None, "slab", None),
        P("mode", None, "slab", None),
        P(None, None, "slab", None, None),
        P(None, None, None, "slab"),
        P(None, "slab"),
        P(),
    )
    out_specs = P("mode", None, "slab", None)
    return jax.shard_map(body, mesh=mesh, in_specs=in_specs, out_specs=out_specs, check_vma=False)
```

```python
import functools

import jax
import jax.numpy as jnp
from jax import lax
from jax.experimental import pallas as pl
from jax.experimental.pallas import tpu as pltpu
from jax.sharding import PartitionSpec as P

NH = 8
HSTEP = 6
ITERS = 2
HALF = NH // 2
OFFS = [HSTEP * (k - HALF) if k < HALF else HSTEP * (k - HALF + 1) for k in range(NH)]
HOPS = 3
CHUNKS = 4
MESH = pl.DeviceIdType.MESH


def kernel(
    n_mode, n_slab,
    edge_ref, rhs_ref, start_ref, mat_ref, coef_ref, out_ref,
    frozen, halo, coef_b, col_b, trans, tails, rows_out, rows_in,
    base, acc_a, acc_b, mixed, edge_v, edge_j,
    halo_send, halo_recv, trans_send, trans_recv, tail_send, tail_recv, row_send, row_recv,
):
    modes = rhs_ref.shape[0]
    nrow = rhs_ref.shape[1]
    nvar = edge_ref.shape[0]
    rad = nrow // nvar
    part = modes // CHUNKS
    me = lax.axis_index("mode")
    slab = lax.axis_index("slab")
    lane = lax.broadcasted_iota(jnp.int32, (1, 128), 1)
    sign = jnp.where(lane < 64, -1.0, 1.0).astype(jnp.float32)

    def turn(x):
        return pltpu.roll(x, 64, x.ndim - 1) * sign

    barrier = pltpu.get_barrier_semaphore()
    for other in range(n_slab):
        @pl.when(other != slab)
        def _():
            pl.semaphore_signal(barrier, inc=1, device_id={"slab": other}, device_id_type=MESH)

    @pl.when(me > 0)
    def _():
        pl.semaphore_signal(barrier, inc=1, device_id={"mode": me - 1}, device_id_type=MESH)

    @pl.when(me < n_mode - 1)
    def _():
        pl.semaphore_signal(barrier, inc=1, device_id={"mode": me + 1}, device_id_type=MESH)

    frozen[0] = start_ref[...].astype(jnp.bfloat16)
    for v in range(nvar):
        rows_out[0, v] = start_ref[:, v * rad, :]

    n_near = jnp.where(me > 0, 1, 0) + jnp.where(me < n_mode - 1, 1, 0)
    pl.semaphore_wait(barrier, n_slab - 1 + n_near)

    def halo_copy(it, way, hop, c):
        cut = pl.ds(c * part, part)
        src = frozen.at[it, cut] if hop == 0 else halo.at[it, way, hop - 1, cut]
        to = me + 1 if way == 0 else me - 1
        return pltpu.make_async_remote_copy(
            src_ref=src,
            dst_ref=halo.at[it, way, hop, cut],
            send_sem=halo_send.at[it, way, hop, c],
            recv_sem=halo_recv.at[it, way, hop, c],
            device_id={"mode": to},
            device_id_type=MESH,
        )

    def sends(way, hop):
        if way == 0:
            return (me < n_mode - 1) & (me >= hop)
        return (me > 0) & (me + hop < n_mode)

    def gets(way, hop):
        return me >= hop + 1 if way == 0 else me + hop + 1 < n_mode

    def halo_start(it, hop, c, way):
        @pl.when(sends(way, hop))
        def _():
            halo_copy(it, way, hop, c).start()

    def halo_wait(it, hop, c, way):
        @pl.when(gets(way, hop))
        def _():
            halo_copy(it, way, hop, c).wait_recv()

    def row_copy(it):
        return pltpu.make_async_remote_copy(
            src_ref=rows_out.at[it], dst_ref=rows_in.at[it],
            send_sem=row_send.at[it], recv_sem=row_recv.at[it],
            device_id={"slab": slab - 1}, device_id_type=MESH,
        )

    def trans_copy(source, other):
        return pltpu.make_async_remote_copy(
            src_ref=trans.at[source], dst_ref=trans.at[source],
            send_sem=trans_send.at[other], recv_sem=trans_recv.at[source],
            device_id={"slab": other}, device_id_type=MESH,
        )

    def tail_copy(it, source, other):
        return pltpu.make_async_remote_copy(
            src_ref=tails.at[it, source], dst_ref=tails.at[it, source],
            send_sem=tail_send.at[it, other], recv_sem=tail_recv.at[it, source],
            device_id={"slab": other}, device_id_type=MESH,
        )

    for c in range(CHUNKS):
        for way in range(2):
            halo_start(0, 0, c, way)

    @pl.when(slab > 0)
    def _():
        row_copy(0).start()

    for v in range(nvar):
        for p in range(2):
            col = mat_ref[p * nrow:(p + 1) * nrow, v * rad:v * rad + 1].astype(jnp.float32)
            col_b[p, v] = jnp.broadcast_to(col * edge_ref[v, 0], (nrow, 128))
    for p in range(2):
        for v in range(nvar):
            for w in range(nvar):
                row = v * rad + rad - 1
                trans[slab, pl.ds(p * nvar * nvar + v * nvar + w, 1)] = -col_b[p, w, row:row + 1, :]
    for other in range(1, n_slab):
        @pl.when(other > slab)
        def _():
            trans_copy(slab, other).start()
    for p in range(2):
        for k in range(NH):
            pick = coef_ref[:, p * NH + k:p * NH + k + 1]
            coef_b[p, k] = jnp.broadcast_to(pick, (nrow, 128))
    for it in range(ITERS):
        for hop in range(HOPS):
            for way in range(2):
                @pl.when(jnp.logical_not(gets(way, hop)))
                def _():
                    halo[it, way, hop] = jnp.zeros(halo.shape[3:], halo.dtype)

    @pl.when(slab == n_slab - 1)
    def _():
        rows_in[...] = jnp.zeros_like(rows_in)

    def product(x):
        both = jnp.dot(mat_ref[...], x, preferred_element_type=jnp.float32)
        return both[:nrow] + turn(both[nrow:])

    def accumulate(it, stage):
        def block(v, carry):
            cut = pl.ds(pl.multiple_of(v * rad, rad), rad)
            for m in range(modes):
                a = b = None
                if stage > 1:
                    a, b = acc_a[m, cut], acc_b[m, cut]
                for k in range(NH):
                    dist, src = divmod(m - OFFS[k], modes)
                    if max(1, abs(dist)) != stage:
                        continue
                    if dist == 0:
                        x = frozen[it, src, cut]
                    else:
                        x = halo[it, 0 if dist < 0 else 1, abs(dist) - 1, src, cut]
                    x = x.astype(jnp.float32)
                    ax, bx = coef_b[0, k, cut] * x, coef_b[1, k, cut] * x
                    a = ax if a is None else a + ax
                    b = bx if b is None else b + bx
                if stage == HOPS:
                    mixed[m, cut] = (a + turn(b)).astype(jnp.bfloat16)
                else:
                    acc_a[m, cut] = a
                    acc_b[m, cut] = b
            return carry

        lax.fori_loop(0, nvar, block, 0)

    last = lax.broadcasted_iota(jnp.int32, (rad, 1), 0) == rad - 1

    for it in range(ITERS):
        @pl.when(slab < n_slab - 1)
        def _():
            row_copy(it).wait_recv()

        for m in range(modes):
            pieces = []
            for v in range(nvar):
                x = rhs_ref[m, v * rad:(v + 1) * rad, :]
                nxt = edge_ref[v, rad - 1] * rows_in[it, v, m:m + 1, :]
                pieces.append(jnp.where(last, x + nxt, x).astype(jnp.bfloat16))
            base[m] = product(jnp.concatenate(pieces, axis=0))

        for hop in range(HOPS):
            for c in range(CHUNKS):
                for way in range(2):
                    halo_wait(it, hop, c, way)
                    if hop + 1 < HOPS:
                        halo_start(it, hop + 1, c, way)
            accumulate(it, hop + 1)

        for m in range(modes):
            base[m] = base[m] - product(mixed[m])
        ends = [base[:, v * rad + rad - 1, :] for v in range(nvar)]
        tails[it, slab] = jnp.concatenate(ends, axis=0).astype(jnp.bfloat16)
        for other in range(n_slab - 1, 0, -1):
            @pl.when(other > slab)
            def _():
                tail_copy(it, slab, other).start()

        def carry_on(j, edge):
            if it == 0:
                trans_copy(j, slab).wait_recv()
            tail_copy(it, j, slab).wait_recv()
            turned = [turn(e) for e in edge]
            fresh = []
            sent = tails[it, j].astype(jnp.float32)
            for v in range(nvar):
                total = sent[v * modes:(v + 1) * modes]
                for w in range(nvar):
                    at = v * nvar + w
                    total = total + trans[j, pl.ds(at, 1)] * edge[w]
                    total = total + trans[j, pl.ds(nvar * nvar + at, 1)] * turned[w]
                fresh.append(total)
            return tuple(fresh)

        zero = jnp.zeros((modes, 128), jnp.float32)
        edge = lax.fori_loop(0, slab, carry_on, (zero,) * nvar)
        for w in range(nvar):
            edge_v[w] = edge[w]
            edge_j[w] = turn(edge[w])
        for m in range(modes):
            total = base[m]
            for w in range(nvar):
                total = total - col_b[0, w] * edge_v[w, m:m + 1, :]
                total = total - col_b[1, w] * edge_j[w, m:m + 1, :]
            if it == ITERS - 1:
                out_ref[m] = total
            else:
                frozen[it + 1, m] = total.astype(jnp.bfloat16)
                for v in range(nvar):
                    rows_out[it + 1, v, m:m + 1, :] = total[v * rad:v * rad + 1, :]
                if (m + 1) % part == 0:
                    for way in range(2):
                        halo_start(it + 1, 0, m // part, way)
        if it < ITERS - 1:
            @pl.when(slab > 0)
            def _():
                row_copy(it + 1).start()

    for other in range(1, n_slab):
        @pl.when(other > slab)
        def _():
            trans_copy(slab, other).wait_send()
            for it in range(ITERS):
                tail_copy(it, slab, other).wait_send()

    @pl.when(slab > 0)
    def _():
        for it in range(ITERS):
            row_copy(it).wait_send()

    for it in range(ITERS):
        for way in range(2):
            for hop in range(HOPS):
                @pl.when(sends(way, hop))
                def _():
                    for c in range(CHUNKS):
                        halo_copy(it, way, hop, c).wait_send()


def body(rhs, start_state, precond, coupling, edge_coef, harm_order):
    n_mode, n_slab = lax.axis_size("mode"), lax.axis_size("slab")
    modes, nvar, rad, cols = rhs.shape
    nrow = nvar * rad
    chosen = harm_order[None, :] == jnp.arange(NH)[:, None]
    ranked = jnp.sum(
        jnp.where(chosen[None, :, :, None, None], coupling[:, None], 0.0), axis=2
    )
    coefs = ranked.transpose(2, 3, 0, 1).reshape(nrow, 2 * NH)
    matrix = precond.reshape(2 * nrow, nrow)
    f32, bf16 = jnp.float32, jnp.bfloat16
    dma = pltpu.SemaphoreType.DMA
    vmem = pl.BlockSpec(memory_space=pltpu.VMEM)
    state = pl.pallas_call(
        functools.partial(kernel, n_mode, n_slab),
        out_shape=jax.ShapeDtypeStruct((modes, nrow, cols), f32),
        in_specs=[pl.BlockSpec(memory_space=pltpu.SMEM)] + [vmem] * 4,
        out_specs=vmem,
        scratch_shapes=[
            pltpu.VMEM((ITERS, modes, nrow, cols), bf16),
            pltpu.VMEM((ITERS, 2, HOPS, modes, nrow, cols), bf16),
            pltpu.VMEM((2, NH, nrow, 128), f32),
            pltpu.VMEM((2, nvar, nrow, 128), f32),
            pltpu.VMEM((n_slab, 56, 128), f32),
            pltpu.VMEM((ITERS, n_slab, nvar * modes, cols), bf16),
            pltpu.VMEM((ITERS, nvar, modes, cols), f32),
            pltpu.VMEM((ITERS, nvar, modes, cols), f32),
            pltpu.VMEM((modes, nrow, cols), f32),
            pltpu.VMEM((modes, nrow, cols), f32),
            pltpu.VMEM((modes, nrow, cols), f32),
            pltpu.VMEM((modes, nrow, cols), bf16),
            pltpu.VMEM((nvar, modes, cols), f32),
            pltpu.VMEM((nvar, modes, cols), f32),
            dma((ITERS, 2, HOPS, CHUNKS)),
            dma((ITERS, 2, HOPS, CHUNKS)),
            dma((n_slab,)),
            dma((n_slab,)),
            dma((ITERS, n_slab)),
            dma((ITERS, n_slab)),
            dma((ITERS,)),
            dma((ITERS,)),
        ],
        compiler_params=pltpu.CompilerParams(
            collective_id=0, has_side_effects=True, vmem_limit_bytes=48 * 1024 * 1024
        ),
    )(edge_coef, rhs.reshape(modes, nrow, cols), start_state.reshape(modes, nrow, cols), matrix, coefs)
    return state.reshape(rhs.shape)


def solution(mesh):
    in_specs = (
        P("mode", None, "slab", None),
        P("mode", None, "slab", None),
        P(None, None, "slab", None, None),
        P(None, None, None, "slab"),
        P(None, "slab"),
        P(),
    )
    out_specs = P("mode", None, "slab", None)
    return jax.shard_map(body, mesh=mesh, in_specs=in_specs, out_specs=out_specs, check_vma=False)
```

```python
import functools

import jax
import jax.numpy as jnp
from jax import lax
from jax.experimental import pallas as pl
from jax.experimental.pallas import tpu as pltpu
from jax.sharding import PartitionSpec as P

NH = 8
HSTEP = 6
ITERS = 2
HALF = NH // 2
OFFS = [HSTEP * (k - HALF) if k < HALF else HSTEP * (k - HALF + 1) for k in range(NH)]
HOPS = 3
CHUNKS = 4
MESH = pl.DeviceIdType.MESH


def kernel(
    n_mode, n_slab,
    edge_ref, rhs_ref, start_ref, mat_ref, coef_ref, out_ref,
    frozen, halo, coef_b, col_b, trans, tails, rows_out, rows_in,
    base, acc_a, acc_b, mixed, edge_v, edge_j,
    halo_send, halo_recv, trans_send, trans_recv, tail_send, tail_recv, row_send, row_recv,
):
    modes = rhs_ref.shape[0]
    nrow = rhs_ref.shape[1]
    nvar = edge_ref.shape[0]
    rad = nrow // nvar
    part = modes // CHUNKS
    me = lax.axis_index("mode")
    slab = lax.axis_index("slab")
    lane = lax.broadcasted_iota(jnp.int32, (1, 128), 1)
    sign = jnp.where(lane < 64, -1.0, 1.0).astype(jnp.float32)

    def turn(x):
        return pltpu.roll(x, 64, x.ndim - 1) * sign

    barrier = pltpu.get_barrier_semaphore()
    for other in range(n_slab):
        @pl.when(other != slab)
        def _():
            pl.semaphore_signal(barrier, inc=1, device_id={"slab": other}, device_id_type=MESH)

    @pl.when(me > 0)
    def _():
        pl.semaphore_signal(barrier, inc=1, device_id={"mode": me - 1}, device_id_type=MESH)

    @pl.when(me < n_mode - 1)
    def _():
        pl.semaphore_signal(barrier, inc=1, device_id={"mode": me + 1}, device_id_type=MESH)

    frozen[0] = start_ref[...].astype(jnp.bfloat16)
    for v in range(nvar):
        rows_out[0, v] = start_ref[:, v * rad, :]

    for v in range(nvar):
        for p in range(2):
            col = mat_ref[p * nrow:(p + 1) * nrow, v * rad:v * rad + 1].astype(jnp.float32)
            col_b[p, v] = jnp.broadcast_to(col * edge_ref[v, 0], (nrow, 128))
    for p in range(2):
        for k in range(NH):
            pick = coef_ref[:, p * NH + k:p * NH + k + 1]
            coef_b[p, k] = jnp.broadcast_to(pick, (nrow, 128))

    n_near = jnp.where(me > 0, 1, 0) + jnp.where(me < n_mode - 1, 1, 0)
    pl.semaphore_wait(barrier, n_slab - 1 + n_near)

    def halo_copy(it, way, hop, c):
        cut = pl.ds(c * part, part)
        src = frozen.at[it, cut] if hop == 0 else halo.at[it, way, hop - 1, cut]
        to = me + 1 if way == 0 else me - 1
        return pltpu.make_async_remote_copy(
            src_ref=src,
            dst_ref=halo.at[it, way, hop, cut],
            send_sem=halo_send.at[it, way, hop, c],
            recv_sem=halo_recv.at[it, way, hop, c],
            device_id={"mode": to},
            device_id_type=MESH,
        )

    def sends(way, hop):
        if way == 0:
            return (me < n_mode - 1) & (me >= hop)
        return (me > 0) & (me + hop < n_mode)

    def gets(way, hop):
        return me >= hop + 1 if way == 0 else me + hop + 1 < n_mode

    def halo_start(it, hop, c, way):
        @pl.when(sends(way, hop))
        def _():
            halo_copy(it, way, hop, c).start()

    def halo_wait(it, hop, c, way):
        @pl.when(gets(way, hop))
        def _():
            halo_copy(it, way, hop, c).wait_recv()

    def row_copy(it):
        return pltpu.make_async_remote_copy(
            src_ref=rows_out.at[it], dst_ref=rows_in.at[it],
            send_sem=row_send.at[it], recv_sem=row_recv.at[it],
            device_id={"slab": slab - 1}, device_id_type=MESH,
        )

    def trans_copy(source, other):
        return pltpu.make_async_remote_copy(
            src_ref=trans.at[source], dst_ref=trans.at[source],
            send_sem=trans_send.at[other], recv_sem=trans_recv.at[source],
            device_id={"slab": other}, device_id_type=MESH,
        )

    def tail_copy(it, source, other):
        return pltpu.make_async_remote_copy(
            src_ref=tails.at[it, source], dst_ref=tails.at[it, source],
            send_sem=tail_send.at[it, other], recv_sem=tail_recv.at[it, source],
            device_id={"slab": other}, device_id_type=MESH,
        )

    for c in range(CHUNKS):
        for way in range(2):
            halo_start(0, 0, c, way)

    @pl.when(slab > 0)
    def _():
        row_copy(0).start()

    for p in range(2):
        for v in range(nvar):
            for w in range(nvar):
                row = v * rad + rad - 1
                trans[slab, pl.ds(p * nvar * nvar + v * nvar + w, 1)] = -col_b[p, w, row:row + 1, :]
    for other in range(1, n_slab):
        @pl.when(other > slab)
        def _():
            trans_copy(slab, other).start()
    for it in range(ITERS):
        for hop in range(HOPS):
            for way in range(2):
                @pl.when(jnp.logical_not(gets(way, hop)))
                def _():
                    halo[it, way, hop] = jnp.zeros(halo.shape[3:], halo.dtype)

    @pl.when(slab == n_slab - 1)
    def _():
        rows_in[...] = jnp.zeros_like(rows_in)

    def product(x):
        both = jnp.dot(mat_ref[...], x, preferred_element_type=jnp.float32)
        return both[:nrow] + turn(both[nrow:])

    def accumulate(it, stage):
        def block(v, carry):
            cut = pl.ds(pl.multiple_of(v * rad, rad), rad)
            for m in range(modes):
                a = b = None
                if stage > 1:
                    a, b = acc_a[m, cut], acc_b[m, cut]
                for k in range(NH):
                    dist, src = divmod(m - OFFS[k], modes)
                    if max(1, abs(dist)) != stage:
                        continue
                    if dist == 0:
                        x = frozen[it, src, cut]
                    else:
                        x = halo[it, 0 if dist < 0 else 1, abs(dist) - 1, src, cut]
                    x = x.astype(jnp.float32)
                    ax, bx = coef_b[0, k, cut] * x, coef_b[1, k, cut] * x
                    a = ax if a is None else a + ax
                    b = bx if b is None else b + bx
                if stage == HOPS:
                    mixed[m, cut] = (a + turn(b)).astype(jnp.bfloat16)
                else:
                    acc_a[m, cut] = a
                    acc_b[m, cut] = b
            return carry

        lax.fori_loop(0, nvar, block, 0)

    last = lax.broadcasted_iota(jnp.int32, (rad, 1), 0) == rad - 1

    for it in range(ITERS):
        @pl.when(slab < n_slab - 1)
        def _():
            row_copy(it).wait_recv()

        for m in range(modes):
            pieces = []
            for v in range(nvar):
                x = rhs_ref[m, v * rad:(v + 1) * rad, :]
                nxt = edge_ref[v, rad - 1] * rows_in[it, v, m:m + 1, :]
                pieces.append(jnp.where(last, x + nxt, x).astype(jnp.bfloat16))
            base[m] = product(jnp.concatenate(pieces, axis=0))

        for hop in range(HOPS):
            for c in range(CHUNKS):
                for way in range(2):
                    halo_wait(it, hop, c, way)
                    if hop + 1 < HOPS:
                        halo_start(it, hop + 1, c, way)
            accumulate(it, hop + 1)

        for m in range(modes):
            base[m] = base[m] - product(mixed[m])
        ends = [base[:, v * rad + rad - 1, :] for v in range(nvar)]
        tails[it, slab] = jnp.concatenate(ends, axis=0).astype(jnp.bfloat16)
        for other in range(n_slab - 1, 0, -1):
            @pl.when(other > slab)
            def _():
                tail_copy(it, slab, other).start()

        def carry_on(j, edge):
            if it == 0:
                trans_copy(j, slab).wait_recv()
            tail_copy(it, j, slab).wait_recv()
            edge, turned = edge[:nvar], edge[nvar:]
            fresh, fresh_turned = [], []
            sent = tails[it, j].astype(jnp.float32)
            for v in range(nvar):
                total = sent[v * modes:(v + 1) * modes]
                total_turned = turn(total)
                for w in range(nvar):
                    at = v * nvar + w
                    real, imag = trans[j, pl.ds(at, 1)], trans[j, pl.ds(nvar * nvar + at, 1)]
                    total = total + (real * edge[w] + imag * turned[w])
                    total_turned = total_turned + (real * turned[w] - imag * edge[w])
                fresh.append(total)
                fresh_turned.append(total_turned)
            return tuple(fresh + fresh_turned)

        zero = jnp.zeros((modes, 128), jnp.float32)
        edge = lax.fori_loop(0, slab, carry_on, (zero,) * (2 * nvar))
        for w in range(nvar):
            edge_v[w] = edge[w]
            edge_j[w] = edge[nvar + w]
        for m in range(modes):
            total = base[m]
            for w in range(nvar):
                total = total - col_b[0, w] * edge_v[w, m:m + 1, :]
                total = total - col_b[1, w] * edge_j[w, m:m + 1, :]
            if it == ITERS - 1:
                out_ref[m] = total
            else:
                frozen[it + 1, m] = total.astype(jnp.bfloat16)
                for v in range(nvar):
                    rows_out[it + 1, v, m:m + 1, :] = total[v * rad:v * rad + 1, :]
                if (m + 1) % part == 0:
                    for way in range(2):
                        halo_start(it + 1, 0, m // part, way)
        if it < ITERS - 1:
            @pl.when(slab > 0)
            def _():
                row_copy(it + 1).start()

    for other in range(1, n_slab):
        @pl.when(other > slab)
        def _():
            trans_copy(slab, other).wait_send()
            for it in range(ITERS):
                tail_copy(it, slab, other).wait_send()

    @pl.when(slab > 0)
    def _():
        for it in range(ITERS):
            row_copy(it).wait_send()

    for it in range(ITERS):
        for way in range(2):
            for hop in range(HOPS):
                @pl.when(sends(way, hop))
                def _():
                    for c in range(CHUNKS):
                        halo_copy(it, way, hop, c).wait_send()


def body(rhs, start_state, precond, coupling, edge_coef, harm_order):
    n_mode, n_slab = lax.axis_size("mode"), lax.axis_size("slab")
    modes, nvar, rad, cols = rhs.shape
    nrow = nvar * rad
    chosen = harm_order[None, :] == jnp.arange(NH)[:, None]
    ranked = jnp.sum(
        jnp.where(chosen[None, :, :, None, None], coupling[:, None], 0.0), axis=2
    )
    coefs = ranked.transpose(2, 3, 0, 1).reshape(nrow, 2 * NH)
    matrix = precond.reshape(2 * nrow, nrow)
    f32, bf16 = jnp.float32, jnp.bfloat16
    dma = pltpu.SemaphoreType.DMA
    vmem = pl.BlockSpec(memory_space=pltpu.VMEM)
    state = pl.pallas_call(
        functools.partial(kernel, n_mode, n_slab),
        out_shape=jax.ShapeDtypeStruct((modes, nrow, cols), f32),
        in_specs=[pl.BlockSpec(memory_space=pltpu.SMEM)] + [vmem] * 4,
        out_specs=vmem,
        scratch_shapes=[
            pltpu.VMEM((ITERS, modes, nrow, cols), bf16),
            pltpu.VMEM((ITERS, 2, HOPS, modes, nrow, cols), bf16),
            pltpu.VMEM((2, NH, nrow, 128), f32),
            pltpu.VMEM((2, nvar, nrow, 128), f32),
            pltpu.VMEM((n_slab, 56, 128), f32),
            pltpu.VMEM((ITERS, n_slab, nvar * modes, cols), bf16),
            pltpu.VMEM((ITERS, nvar, modes, cols), f32),
            pltpu.VMEM((ITERS, nvar, modes, cols), f32),
            pltpu.VMEM((modes, nrow, cols), f32),
            pltpu.VMEM((modes, nrow, cols), f32),
            pltpu.VMEM((modes, nrow, cols), f32),
            pltpu.VMEM((modes, nrow, cols), bf16),
            pltpu.VMEM((nvar, modes, cols), f32),
            pltpu.VMEM((nvar, modes, cols), f32),
            dma((ITERS, 2, HOPS, CHUNKS)),
            dma((ITERS, 2, HOPS, CHUNKS)),
            dma((n_slab,)),
            dma((n_slab,)),
            dma((ITERS, n_slab)),
            dma((ITERS, n_slab)),
            dma((ITERS,)),
            dma((ITERS,)),
        ],
        compiler_params=pltpu.CompilerParams(
            collective_id=0, has_side_effects=True, vmem_limit_bytes=48 * 1024 * 1024
        ),
    )(edge_coef, rhs.reshape(modes, nrow, cols), start_state.reshape(modes, nrow, cols), matrix, coefs)
    return state.reshape(rhs.shape)


def solution(mesh):
    in_specs = (
        P("mode", None, "slab", None),
        P("mode", None, "slab", None),
        P(None, None, "slab", None, None),
        P(None, None, None, "slab"),
        P(None, "slab"),
        P(),
    )
    out_specs = P("mode", None, "slab", None)
    return jax.shard_map(body, mesh=mesh, in_specs=in_specs, out_specs=out_specs, check_vma=False)
```
